32 devices in a mesh: subj: 4 (over y, x), slab: 8 (over z, core).
Axes of the slice: x: 2, y: 2, z: 4, core: 2. Of those that a mesh axis runs over, the one named last changes fastest.
Arguments:
- subjects_data: bfloat16 [16384, 16, 512], P('subj', 'slab'), may hold values from -6 to 6
- covariates: bfloat16 [3, 16384], P(None, 'subj'), may hold values from -5 to 5
- permutes: int32 [32, 16384], P(None, 'subj'), may hold values from 0 to 16383, as said below
- brain_mask: int32 [16, 512], P('slab'), may hold values 0 or 1
Outputs:
- smooth_t: float32 [16, 512], P('slab')
- p_values: float32 [16, 512], P('slab')
- perm_peaks: float32 [32], replicated
The draws below stay inside these ranges and needn't reach their ends.
Inputs may be any that keep to these rules, and one draw needn't show every extreme that they name: `permutes`: each row is a permutation of the subjects that maps every aligned block of 256 subjects onto itself.
All inputs are finite; a program needn't handle non-finite values. No bound on the sum of `brain_mask` on one device may be relied on, other than what follows from the above.
Results may differ from the reference program's by a relative error of at most 0.0003.
Values sent between devices are 32-bit elements; how exact they have to be, the bound alone decides.
A program may use at most 64 MiB of HBM per device.

```python
import math
import jax
import jax.numpy as jnp
from jax import lax

BLOCK = 256
PERMS = 32
PX = 16
PY = 32
S = 16384
NZ = 16
PLANE = 512


def draw_permutes(key, part):
    blocks = S // BLOCK
    count_all = PERMS * blocks
    key_list = jax.random.split(key, count_all)

    def shuffle_one(subkey):
        return jax.random.permutation(subkey, BLOCK).astype(jnp.int32)
    perm_rows = jax.vmap(shuffle_one)(key_list)
    offsets = jnp.arange(count_all, dtype=jnp.int32) % blocks * BLOCK
    return (perm_rows + offsets[:, None]).reshape(PERMS, S)


def shared_fields(key):
    base = jax.random.fold_in(key, 7)
    key_offset, key_noise = jax.random.split(base, 2)
    blocks = S // BLOCK
    block_offset = jax.random.uniform(key_offset, (blocks,), jnp.float32, -1.0, 1.0)
    subject_offset = jnp.repeat(block_offset, BLOCK)
    cov_noise = jax.random.normal(key_noise, (3, S), jnp.float32)
    zero_row = jnp.zeros((S,), jnp.float32)
    shifted = cov_noise + jnp.stack([zero_row, subject_offset, zero_row], axis=0)
    return (jnp.clip(shifted, -5.0, 5.0), subject_offset)


def draw_covariates(key, part):
    cov_values, subject_offset = shared_fields(key)
    return cov_values.astype(jnp.bfloat16)


def draw_subjects_data(key, part):
    cov_values, subject_offset = shared_fields(key)
    base = jax.random.fold_in(key, 11)
    key_mean, key_strength, key_region, key_noise = jax.random.split(base, 4)
    voxel_mean = jax.random.uniform(key_mean, (NZ, PLANE), jnp.float32, -0.3, 0.3)
    strength = jax.random.uniform(key_strength, (NZ, PLANE), jnp.float32, 0.0, 0.08)
    region = jax.random.bernoulli(key_region, 0.5, (NZ, PX, 1)).astype(jnp.float32)
    region = jnp.broadcast_to(region, (NZ, PX, PY)).reshape(NZ, PLANE)
    effect = strength * region
    noise = jax.random.normal(key_noise, (S, NZ, PLANE), jnp.float32)
    values = noise + voxel_mean[None] + cov_values[0][:, None, None] * effect[None] + 0.5 * subject_offset[:, None, None]
    return jnp.clip(values, -6.0, 6.0).astype(jnp.bfloat16)


def set_ends(array, key, low, top_value):
    extent = array.shape
    spot = [jax.random.randint(jax.random.fold_in(key, axis), (), 0, extent[axis]) for axis in range(len(extent))]
    array = array.at[tuple(spot)].set(low)
    longest = extent.index(max(extent))
    spot[longest] = (spot[longest] + 1) % extent[longest]
    return array.at[tuple(spot)].set(top_value)


def setup_inputs(seed: int = 0) -> dict:
    keys = jax.random.split(jax.random.key(seed), 5)
    subjects_data = draw_subjects_data(jax.random.fold_in(keys[4], 71), 0)
    covariates = draw_covariates(jax.random.fold_in(keys[4], 71), 0)
    permutes = draw_permutes(jax.random.fold_in(keys[4], 71), 0)
    brain_mask = set_ends((jax.random.randint(keys[3], (NZ, PLANE), 0, 4) < 3).astype(jnp.int32), jax.random.fold_in(keys[3], 1), 0, 1)
    return {"subjects_data": subjects_data, "covariates": covariates, "permutes": permutes, "brain_mask": brain_mask}


gauss_raw = tuple((math.exp(-0.5 * (offset - 2) ** 2) for offset in range(5)))
gauss_taps = tuple((value / sum(gauss_raw) for value in gauss_raw))

def band_weight(gap):
    total = jnp.zeros(gap.shape, jnp.float32)
    for position, weight in enumerate(gauss_taps):
        total = total + weight * (gap == position - 2).astype(jnp.float32)
    return total

def plane_kernel(rows_x, rows_y):
    cell_index = jnp.arange(rows_x * rows_y, dtype=jnp.int32)
    cell_row = cell_index // rows_y
    cell_col = cell_index % rows_y
    row_gap = cell_row[:, None] - cell_row[None, :]
    col_gap = cell_col[:, None] - cell_col[None, :]
    return band_weight(row_gap) * band_weight(col_gap)

def permute_design(permutes, design):
    copies = permutes.shape[0]
    subj_rows = design.shape[1]
    blocks = subj_rows // BLOCK
    local_idx = (permutes % BLOCK).reshape(copies, blocks, BLOCK).transpose(1, 0, 2)
    block_rows = design.reshape(4, blocks, BLOCK).transpose(1, 0, 2)

    def one_block(pair):
        local_part, design_part = pair
        onehot = (local_part[:, :, None] == jnp.arange(BLOCK, dtype=jnp.int32)[None, None, :]).astype(jnp.float32)
        return jnp.einsum('ci,pij->pcj', design_part.astype(jnp.float32), onehot).astype(jnp.bfloat16)
    shuffled = lax.map(one_block, (local_idx, block_rows))
    return shuffled.transpose(1, 2, 0, 3).reshape(copies * 4, subj_rows)

def t_statistics(products, squares, crossed, freedom):
    count_maps = crossed.shape[0] // 4
    width = products.shape[1]
    gram = crossed[0:4]
    chol_z = jnp.linalg.cholesky(gram[1:4, 1:4])
    gamma_fit = jax.scipy.linalg.cho_solve((chol_z, True), products[1:4])
    resid_sq = squares[0] - lax.optimization_barrier(jnp.sum(products[1:4] * gamma_fit, axis=0))
    cross_nuis = crossed.reshape(count_maps, 4, 4)[:, :, 1:4]
    projections = products.reshape(count_maps, 4, width) - jnp.einsum('pkm,mn->pkn', cross_nuis, gamma_fit, precision=lax.Precision.HIGHEST)
    chol_full = jnp.linalg.cholesky(gram)
    inverse = jax.scipy.linalg.cho_solve((chol_full, True), jnp.eye(4, dtype=gram.dtype))
    slope_est = jnp.einsum('k,pkn->pn', inverse[0], projections, precision=lax.Precision.HIGHEST)
    mixed_proj = jnp.einsum('kl,pln->pkn', inverse, projections, precision=lax.Precision.HIGHEST)
    quadratic = lax.optimization_barrier(jnp.sum(projections * mixed_proj, axis=1))
    return slope_est / jnp.sqrt((resid_sq - quadratic) / freedom * inverse[0, 0])

def reference(subjects_data, covariates, permutes, brain_mask):
    ones_row = jnp.ones((1, S), jnp.bfloat16)
    design = jnp.concatenate([covariates[0:1], ones_row, covariates[1:3]], axis=0)
    designs = jnp.concatenate([design, permute_design(permutes, design)], axis=0)
    crossed = jnp.dot(designs.astype(jnp.float32), design.T.astype(jnp.float32), preferred_element_type=jnp.float32)

    def slice_stats(slice_index):
        slice_data = lax.dynamic_index_in_dim(subjects_data, slice_index, 1, keepdims=False)
        products = jnp.dot(designs.astype(jnp.float32), slice_data.astype(jnp.float32), preferred_element_type=jnp.float32)
        squares = lax.optimization_barrier(jnp.sum(jnp.square(slice_data.astype(jnp.float32)), axis=0))[None]
        return t_statistics(products, squares, crossed, S - 4)
    tmaps = lax.map(slice_stats, jnp.arange(NZ, dtype=jnp.int32)).transpose(1, 0, 2)
    mask_float = brain_mask.astype(jnp.float32)
    masked = tmaps * mask_float[None]
    padded = jnp.pad(masked, ((0, 0), (2, 2), (0, 0)))
    depth_smooth = gauss_taps[0] * padded[:, 0:NZ]
    for position in range(1, 5):
        depth_smooth = depth_smooth + gauss_taps[position] * padded[:, position:position + NZ]
    kernel = plane_kernel(PX, PY)
    smoothed = jnp.dot(depth_smooth.reshape(-1, PLANE), kernel, precision=lax.Precision.HIGHEST).reshape(PERMS + 1, NZ, PLANE) * mask_float[None]
    smooth_t = smoothed[0]
    perm_peaks = lax.optimization_barrier(jnp.max(jnp.where(mask_float[None] > 0, smoothed[1:], -1e+30), axis=(1, 2)))
    p_values = mask_float * (1.0 + lax.optimization_barrier(jnp.sum(jax.nn.sigmoid((perm_peaks[:, None, None] - smooth_t[None]) / 0.2), axis=0))) / (PERMS + 1)
    return (smooth_t, p_values, perm_peaks)
```

```python
import functools
import math

import jax
import jax.numpy as jnp
from jax import lax
from jax.experimental import pallas as pl
from jax.experimental.pallas import tpu as pltpu
from jax.sharding import PartitionSpec as P

BLOCK = 256
HALF = 128
PX = 16
PY = 32
LANES = 128
MESH = pl.DeviceIdType.MESH

gauss_raw = tuple((math.exp(-0.5 * (offset - 2) ** 2) for offset in range(5)))
gauss_taps = tuple((value / sum(gauss_raw) for value in gauss_raw))

NT = (((1,), (1,)), ((), ()))


def products_kernel(groups, per, rows, x_ref, cov_ref, perm_ref, chunk_ref, obs_ref, flat, shuf_a, shuf_b, des):
    step = pl.program_id(0)
    copies = perm_ref.shape[0]
    top = groups * rows
    voxels = chunk_ref.shape[2] - LANES
    half_tiles = voxels // (2 * LANES)

    @pl.when(step == 0)
    def _():
        chunk_ref[...] = jnp.zeros_like(chunk_ref)
        obs_ref[...] = jnp.zeros_like(obs_ref)
        shuf_a[...] = jnp.zeros_like(shuf_a)
        shuf_b[...] = jnp.zeros_like(shuf_b)
        des[...] = jnp.zeros_like(des)

    cov = cov_ref[...].astype(jnp.float32)
    des[0:3, :] = cov
    des[4:7, :] = cov
    des[8:9, :] = cov[0:1]
    des[9:10, :] = jnp.ones((1, BLOCK), jnp.float32)
    des[10:12, :] = cov[1:3]
    shuf_a[top : top + 4, :] = des[8:12, 0:HALF]
    shuf_b[top : top + 4, :] = des[8:12, HALF:BLOCK]

    local = perm_ref[...] & (BLOCK - 1)
    high = local // HALF
    low = (local & (HALF - 1)).astype(jnp.float32)
    row_high = lax.broadcasted_iota(jnp.int32, (8, BLOCK), 0) // 4
    place = (
        lax.broadcasted_iota(jnp.int32, (HALF // 16, 16, BLOCK), 0) * 16
        + lax.broadcasted_iota(jnp.int32, (HALF // 16, 16, BLOCK), 1)
    ).astype(jnp.float32).astype(jnp.bfloat16)
    one = jnp.ones((), jnp.bfloat16)
    zero = jnp.zeros((), jnp.bfloat16)
    base = des[0:8, :]
    for pair in range(copies // 2):
        lefts = []
        hots = []
        for p in (2 * pair, 2 * pair + 1):
            lefts.append(jnp.where(high[p : p + 1] == row_high, base, 0.0))
            spread = jnp.broadcast_to(low[p : p + 1], (16, BLOCK)).astype(jnp.bfloat16)
            hots.append(jnp.where(spread[None] == place, one, zero).reshape(HALF, BLOCK))
        left = jnp.concatenate(lefts, axis=0).astype(jnp.bfloat16)
        hot = jnp.concatenate(hots, axis=0)
        moved = lax.dot_general(left, hot, NT, preferred_element_type=jnp.float32)
        for side in range(2):
            p = 2 * pair + side
            row = p // per * rows + p % per
            part = moved[8 * side : 8 * side + 8, HALF * side : HALF * side + HALF]
            shuf_a[pl.ds(row, 3, stride=per), :] = part[0:3]
            shuf_b[pl.ds(row, 3, stride=per), :] = part[4:7]

    flat[...] = x_ref[...].astype(jnp.float32)
    designs = jnp.concatenate([shuf_a[...], shuf_b[...]], axis=1).astype(jnp.bfloat16)
    for tile in range(half_tiles):
        z = tile // (half_tiles // 2)
        cells = [2 * (tile % (half_tiles // 2)) + i for i in range(2)]
        part = jnp.concatenate(
            [flat[pl.ds(2 * c + z, BLOCK, stride=8), :] for c in cells], axis=1
        )
        cols = slice(2 * LANES * tile, 2 * LANES * (tile + 1))
        res = jnp.dot(designs, part.astype(jnp.bfloat16), preferred_element_type=jnp.float32)
        for g in range(groups):
            chunk_ref[g, :, cols] += res[g * rows : (g + 1) * rows]
        squares = jnp.sum(part * part, axis=0, keepdims=True)
        sub = lax.broadcasted_iota(jnp.int32, (8, 2 * LANES), 0)
        obs_ref[:, cols] += res[top : top + 8] + jnp.where(sub == 4, squares, 0.0)
    right = jnp.concatenate(
        [des[8:16, :], jnp.zeros((LANES - 8, BLOCK), jnp.float32)], axis=0
    ).astype(jnp.bfloat16)
    res = lax.dot_general(designs, right, NT, preferred_element_type=jnp.float32)
    for g in range(groups):
        chunk_ref[g, :, voxels:] += res[g * rows : (g + 1) * rows]
    obs_ref[:, voxels:] += res[top : top + 8]


def cholesky(mat):
    size = len(mat)
    low = [[None] * size for _ in range(size)]
    for j in range(size):
        total = mat[j][j]
        for k in range(j):
            total = total - low[j][k] * low[j][k]
        low[j][j] = jnp.sqrt(total)
        for i in range(j + 1, size):
            total = mat[i][j]
            for k in range(j):
                total = total - low[i][k] * low[j][k]
            low[i][j] = total / low[j][j]
    return low


def cho_solve(low, inv_diag, rhs):
    size = len(low)
    half = []
    for i in range(size):
        total = rhs[i]
        for k in range(i):
            total = total - low[i][k] * half[k]
        half.append(total * inv_diag[i])
    out = [None] * size
    for i in reversed(range(size)):
        total = half[i]
        for k in range(i + 1, size):
            total = total - low[k][i] * out[k]
        out[i] = total * inv_diag[i]
    return out


def blur(cells, stride, coord, size):
    width = cells.shape[1]
    total = None
    for position in range(5):
        d = position - 2
        moved = cells if d == 0 else pltpu.roll(cells, (-d * stride) % width, 1)
        inside = (coord + d >= 0) & (coord + d < size)
        term = gauss_taps[position] * jnp.where(inside, moved, 0.0)
        total = term if total is None else total + term
    return total


def maps_kernel(
    n, m, per, copies, freedom,
    chunk_ref, obs_ref, mask_ref, smooth_ref, pval_ref, peak_ref,
    got, gobs, own, own_o, low, low_o, high, high_o, field, pk1, pk2,
    send, recv, send_o, recv_o, hsend, hrecv, psend, prec, qsend, qrec,
):
    me = lax.axis_index("subj")
    slab = lax.axis_index("slab")
    plane = mask_ref.shape[1]
    voxels = 2 * plane

    barrier = pltpu.get_barrier_semaphore()
    for o in range(1, n):
        pl.semaphore_signal(barrier, inc=1, device_id=(lax.rem(me + o, n), slab), device_id_type=MESH)
    for o in range(1, m):
        pl.semaphore_signal(barrier, inc=1, device_id=(me, lax.rem(slab + o, m)), device_id_type=MESH)
    pl.semaphore_wait(barrier, n + m - 2)

    copies_a = []
    for o in range(1, n):
        to = lax.rem(me + o, n)
        copies_a.append(pltpu.make_async_remote_copy(
            src_ref=obs_ref, dst_ref=gobs.at[o], send_sem=send_o.at[o], recv_sem=recv_o.at[o],
            device_id=(to, slab), device_id_type=MESH))
        copies_a[-1].start()
    copies_b = []
    for o in range(1, n):
        to = lax.rem(me + o, n)
        copies_b.append(pltpu.make_async_remote_copy(
            src_ref=chunk_ref.at[to], dst_ref=got.at[o], send_sem=send.at[o], recv_sem=recv.at[o],
            device_id=(to, slab), device_id_type=MESH))
        copies_b[-1].start()
    got[0] = chunk_ref[me]
    gobs[0] = obs_ref[...]

    cells = mask_ref[...].astype(jnp.float32)
    mask_row = jnp.concatenate([cells[0:1], cells[1:2]], axis=1)

    for copy in copies_a:
        copy.wait()
    obs = gobs[lax.rem(me + n, n)]
    for s in range(1, n):
        obs = obs + gobs[lax.rem(me - s + n, n)]
    prod = [obs[k : k + 1, :voxels] for k in range(4)]
    gram = [[obs[i : i + 1, voxels + j : voxels + j + 1] for j in range(4)] for i in range(4)]
    low_z = cholesky([row[1:4] for row in gram[1:4]])
    fit = cho_solve(low_z, [1.0 / low_z[i][i] for i in range(3)], prod[1:4])
    resid = obs[4:5, :voxels] - (prod[1] * fit[0] + prod[2] * fit[1] + prod[3] * fit[2])
    low_f = cholesky(gram)
    inv_diag = [1.0 / low_f[i][i] for i in range(4)]
    unit = [jnp.zeros((1, 1), jnp.float32), jnp.ones((1, 1), jnp.float32)]
    columns = [cho_solve(low_f, inv_diag, [unit[int(i == j)] for i in range(4)]) for j in range(4)]
    inverse = [[columns[j][i] for j in range(4)] for i in range(4)]

    def statistic(proj):
        slope = sum(inverse[0][k] * proj[k] for k in range(4))
        quad = sum(proj[k] * sum(inverse[k][l] * proj[l] for l in range(4)) for k in range(4))
        return slope / jnp.sqrt((resid - quad) / freedom * inverse[0][0])

    seen = [
        prod[k] - sum(gram[k][1 + i] * fit[i] for i in range(3)) for k in range(4)
    ]
    own_o[...] = statistic(seen) * mask_row

    for copy in copies_b:
        copy.wait()
    chunk = got[0]
    for o in range(1, n):
        chunk = chunk + got[o]
    proj = []
    for c in range(3):
        rows = chunk[c * per : (c + 1) * per]
        proj.append(
            rows[:, :voxels]
            - sum(rows[:, voxels + 1 + i : voxels + 2 + i] * fit[i] for i in range(3))
        )
    own[...] = statistic([proj[0], seen[1], proj[1], proj[2]]) * mask_row

    up = (me, lax.rem(slab + 1, m))
    down = (me, lax.rem(slab + m - 1, m))

    def halo(src, dst, k, to):
        return pltpu.make_async_remote_copy(
            src_ref=src, dst_ref=dst, send_sem=hsend.at[k], recv_sem=hrecv.at[k],
            device_id=to, device_id_type=MESH)

    rise = [halo(own, low, 0, up), halo(own_o, low_o, 1, up)]
    fall = [halo(own, high, 2, down), halo(own_o, high_o, 3, down)]

    @pl.when(slab < m - 1)
    def _():
        for copy in rise:
            copy.start()

    @pl.when(slab > 0)
    def _():
        for copy in fall:
            copy.start()

    @pl.when(slab == 0)
    def _():
        low[...] = jnp.zeros_like(low)
        low_o[...] = jnp.zeros_like(low_o)

    @pl.when(slab == m - 1)
    def _():
        high[...] = jnp.zeros_like(high)
        high_o[...] = jnp.zeros_like(high_o)

    field[...] = jnp.zeros_like(field)

    @pl.when(slab > 0)
    def _():
        for copy in rise:
            copy.wait_recv()

    @pl.when(slab < m - 1)
    def _():
        for copy in fall:
            copy.wait_recv()

    def deep(lower, mine, upper):
        slices = []
        for ref in (lower, mine, upper):
            value = ref[...]
            slices += [value[:, :plane], value[:, plane:]]
        return [
            sum(gauss_taps[position] * slices[position + z] for position in range(5))
            for z in range(2)
        ]

    first, second = deep(low, own, high)
    field[0:per, :] = first
    field[8 : 8 + per, :] = second
    first, second = deep(low_o, own_o, high_o)
    field[16:17, :] = first
    field[17:18, :] = second

    cell = lax.broadcasted_iota(jnp.int32, (24, plane), 1)
    smooth = blur(field[...], PY, cell // PY, PX)
    smooth = blur(smooth, 1, cell % PY, PY)

    peaks = jnp.maximum(
        jnp.max(jnp.where(cells[0:1] > 0, smooth[0:per] * cells[0:1], -1e30), axis=1, keepdims=True),
        jnp.max(jnp.where(cells[1:2] > 0, smooth[8 : 8 + per] * cells[1:2], -1e30), axis=1, keepdims=True),
    )
    pk1[0] = jnp.broadcast_to(peaks, (per, LANES))
    copies_p = []
    for o in range(1, m):
        copies_p.append(pltpu.make_async_remote_copy(
            src_ref=pk1.at[0], dst_ref=pk1.at[o], send_sem=psend.at[o], recv_sem=prec.at[o],
            device_id=(me, lax.rem(slab + o, m)), device_id_type=MESH))
        copies_p[-1].start()
    seen_t = [smooth[16 + z : 17 + z] * cells[z : z + 1] for z in range(2)]
    smooth_ref[...] = jnp.concatenate(seen_t, axis=0)
    seen_row = jnp.concatenate(seen_t, axis=1)

    for copy in copies_p:
        copy.wait_recv()
    best = pk1[0]
    for o in range(1, m):
        best = jnp.maximum(best, pk1[o])
    pk2[0] = best
    copies_q = []
    for o in range(1, n):
        copies_q.append(pltpu.make_async_remote_copy(
            src_ref=pk2.at[0], dst_ref=pk2.at[o], send_sem=qsend.at[o], recv_sem=qrec.at[o],
            device_id=(lax.rem(me + o, n), slab), device_id_type=MESH))
        copies_q[-1].start()
    for copy in copies_q:
        copy.wait_recv()

    count = jnp.zeros((1, voxels), jnp.float32)
    line = jnp.zeros((1, LANES), jnp.float32)
    sub = lax.broadcasted_iota(jnp.int32, (per, LANES), 0)
    lane = lax.broadcasted_iota(jnp.int32, (per, LANES), 1)
    for d in range(n):
        value = pk2[lax.rem(me - d + n, n)]
        level = jax.nn.sigmoid((value[:, 0:1] - seen_row) / 0.2)
        count = count + jnp.sum(level, axis=0, keepdims=True)
        line = line + jnp.sum(jnp.where(lane == sub + d * per, value, 0.0), axis=0, keepdims=True)
    pval = mask_row * (1.0 + count) / (copies + 1)
    pval_ref[...] = jnp.concatenate([pval[:, :plane], pval[:, plane:]], axis=0)
    peak_ref[...] = line[:, :copies]

    for copy in copies_p + copies_q:
        copy.wait_send()

    @pl.when(slab < m - 1)
    def _():
        for copy in rise:
            copy.wait_send()

    @pl.when(slab > 0)
    def _():
        for copy in fall:
            copy.wait_send()


def body(n, m, subjects_data, covariates, permutes, brain_mask):
    subj_rows, depth, plane = subjects_data.shape
    assert depth == 2 and plane == PX * PY
    copies = permutes.shape[0]
    per = copies // n
    rows = -(-3 * per // 8) * 8
    voxels = depth * plane
    width = voxels + LANES
    tiles = plane // LANES
    flat_rows = depth * tiles
    data = (
        subjects_data.reshape(subj_rows, depth, tiles, LANES)
        .transpose(0, 2, 1, 3)
        .reshape(subj_rows * flat_rows, LANES)
    )
    height = -(-(n * rows + 8) // 16) * 16
    f32 = jnp.float32
    chunk, obs = pl.pallas_call(
        functools.partial(products_kernel, n, per, rows),
        grid=(subj_rows // BLOCK,),
        in_specs=[
            pl.BlockSpec((BLOCK * flat_rows, LANES), lambda b: (b, 0)),
            pl.BlockSpec((3, BLOCK), lambda b: (0, b)),
            pl.BlockSpec((copies, BLOCK), lambda b: (0, b)),
        ],
        out_specs=[
            pl.BlockSpec((n, rows, width), lambda b: (0, 0, 0)),
            pl.BlockSpec((8, width), lambda b: (0, 0)),
        ],
        out_shape=[
            jax.ShapeDtypeStruct((n, rows, width), f32),
            jax.ShapeDtypeStruct((8, width), f32),
        ],
        scratch_shapes=[
            pltpu.VMEM((BLOCK * flat_rows, LANES), f32),
            pltpu.VMEM((height, HALF), f32),
            pltpu.VMEM((height, HALF), f32),
            pltpu.VMEM((16, BLOCK), f32),
        ],
        compiler_params=pltpu.CompilerParams(vmem_limit_bytes=60 * 2**20),
        name="products",
    )(data, covariates, permutes)

    vmem = pl.BlockSpec(memory_space=pltpu.VMEM)
    dma = pltpu.SemaphoreType.DMA
    smooth_t, p_values, peaks = pl.pallas_call(
        functools.partial(maps_kernel, n, m, per, copies, float(n * subj_rows - 4)),
        in_specs=[vmem] * 3,
        out_specs=[vmem] * 3,
        out_shape=[
            jax.ShapeDtypeStruct((depth, plane), f32),
            jax.ShapeDtypeStruct((depth, plane), f32),
            jax.ShapeDtypeStruct((1, copies), f32),
        ],
        scratch_shapes=[
            pltpu.VMEM((n, rows, width), f32),
            pltpu.VMEM((n, 8, width), f32),
            pltpu.VMEM((per, voxels), f32),
            pltpu.VMEM((1, voxels), f32),
            pltpu.VMEM((per, voxels), f32),
            pltpu.VMEM((1, voxels), f32),
            pltpu.VMEM((per, voxels), f32),
            pltpu.VMEM((1, voxels), f32),
            pltpu.VMEM((24, plane), f32),
            pltpu.VMEM((m, per, LANES), f32),
            pltpu.VMEM((n, per, LANES), f32),
            dma((n,)), dma((n,)), dma((n,)), dma((n,)),
            dma((4,)), dma((4,)), dma((m,)), dma((m,)), dma((n,)), dma((n,)),
        ],
        compiler_params=pltpu.CompilerParams(
            collective_id=0, has_side_effects=True, vmem_limit_bytes=32 * 2**20
        ),
        name="maps",
    )(chunk, obs, brain_mask)
    return smooth_t, p_values, peaks.reshape(copies)


def solution(mesh):
    return jax.shard_map(
        functools.partial(body, mesh.shape["subj"], mesh.shape["slab"]),
        mesh=mesh,
        in_specs=(P("subj", "slab", None), P(None, "subj"), P(None, "subj"), P("slab", None)),
        out_specs=(P("slab", None), P("slab", None), P()),
        check_vma=False,
    )
```

```python
import functools
import math

import jax
import jax.numpy as jnp
from jax import lax
from jax.experimental import pallas as pl
from jax.experimental.pallas import tpu as pltpu
from jax.sharding import PartitionSpec as P

BLOCK = 256
HALF = 128
PX = 16
PY = 32
LANES = 128
MESH = pl.DeviceIdType.MESH

gauss_raw = tuple((math.exp(-0.5 * (offset - 2) ** 2) for offset in range(5)))
gauss_taps = tuple((value / sum(gauss_raw) for value in gauss_raw))

NT = (((1,), (1,)), ((), ()))


def cholesky(mat):
    size = len(mat)
    low = [[None] * size for _ in range(size)]
    for j in range(size):
        total = mat[j][j]
        for k in range(j):
            total = total - low[j][k] * low[j][k]
        low[j][j] = jnp.sqrt(total)
        for i in range(j + 1, size):
            total = mat[i][j]
            for k in range(j):
                total = total - low[i][k] * low[j][k]
            low[i][j] = total / low[j][j]
    return low


def cho_solve(low, inv_diag, rhs):
    size = len(low)
    half = []
    for i in range(size):
        total = rhs[i]
        for k in range(i):
            total = total - low[i][k] * half[k]
        half.append(total * inv_diag[i])
    out = [None] * size
    for i in reversed(range(size)):
        total = half[i]
        for k in range(i + 1, size):
            total = total - low[k][i] * out[k]
        out[i] = total * inv_diag[i]
    return out


def blur(cells, stride, coord, size):
    width = cells.shape[1]
    total = None
    for position in range(5):
        d = position - 2
        moved = cells if d == 0 else pltpu.roll(cells, (-d * stride) % width, 1)
        inside = (coord + d >= 0) & (coord + d < size)
        term = gauss_taps[position] * jnp.where(inside, moved, 0.0)
        total = term if total is None else total + term
    return total


def maps_kernel(
    n, m, per, freedom,
    x_hbm, cov_hbm, perm_hbm, mask_hbm, smooth_ref, peak_ref,
    raw, cov_ref, perm_ref, mask_ref, flat, shuf_a, shuf_b, des, des_all, designs,
    out_x, got_x, out, got, own, own_o, low, low_o, high, high_o, field, pk1, pk2,
    xsem, csem, xsend, xrecv, send, recv, hsend, hrecv, psend, prec, qsend, qrec,
):
    me = lax.axis_index("subj")
    slab = lax.axis_index("slab")
    plane = mask_ref.shape[1]
    copies = perm_ref.shape[0]
    rows = out.shape[2] - 8
    top = n * rows
    wide = out.shape[3]
    tiles = out.shape[0]
    blocks = perm_ref.shape[1] // BLOCK
    flat_rows = raw.shape[0] // perm_ref.shape[1]
    span = BLOCK * flat_rows

    small = [
        pltpu.make_async_copy(src, dst, csem.at[i])
        for i, (src, dst) in enumerate(((perm_hbm, perm_ref), (cov_hbm, cov_ref), (mask_hbm, mask_ref)))
    ]
    for copy in small:
        copy.start()

    def load(b):
        at = pl.ds(pl.multiple_of(b * span, span), span)
        return pltpu.make_async_copy(x_hbm.at[at], raw.at[at], xsem.at[b])

    def start_load(b, carry):
        load(b).start()
        return carry

    lax.fori_loop(0, blocks, start_load, 0)

    barrier = pltpu.get_barrier_semaphore()
    for o in range(1, n):
        pl.semaphore_signal(barrier, inc=1, device_id=(lax.rem(me + o, n), slab), device_id_type=MESH)
    for o in range(1, m):
        pl.semaphore_signal(barrier, inc=1, device_id=(me, lax.rem(slab + o, m)), device_id_type=MESH)

    shuf_a[...] = jnp.zeros_like(shuf_a)
    shuf_b[...] = jnp.zeros_like(shuf_b)
    des[...] = jnp.zeros_like(des)
    out_x[...] = jnp.zeros_like(out_x)
    for copy in small:
        copy.wait()

    row_high = lax.broadcasted_iota(jnp.int32, (8, BLOCK), 0) // 4
    one = jnp.ones((), jnp.bfloat16)
    zero = jnp.zeros((), jnp.bfloat16)

    def shuffle(b, carry):
        at = pl.ds(pl.multiple_of(b * BLOCK, BLOCK), BLOCK)
        place = (
            lax.broadcasted_iota(jnp.int32, (HALF // 16, 16, BLOCK), 0) * 16
            + lax.broadcasted_iota(jnp.int32, (HALF // 16, 16, BLOCK), 1)
        ).astype(jnp.float32).astype(jnp.bfloat16)
        cov = cov_ref[:, at].astype(jnp.float32)
        des[0:3, :] = cov
        des[4:7, :] = cov
        des[8:9, :] = cov[0:1]
        des[9:10, :] = jnp.ones((1, BLOCK), jnp.float32)
        des[10:12, :] = cov[1:3]
        shuf_a[top : top + 4, :] = des[8:12, 0:HALF]
        shuf_b[top : top + 4, :] = des[8:12, HALF:BLOCK]
        des_all[:, at] = des[8:24, :].astype(jnp.bfloat16)

        local = perm_ref[:, at] & (BLOCK - 1)
        upper = local // HALF
        lower = (local & (HALF - 1)).astype(jnp.float32)
        base = des[0:8, :]
        for pair in range(copies // 2):
            lefts = []
            hots = []
            for p in (2 * pair, 2 * pair + 1):
                lefts.append(jnp.where(upper[p : p + 1] == row_high, base, 0.0))
                spread = jnp.broadcast_to(lower[p : p + 1], (16, BLOCK)).astype(jnp.bfloat16)
                hots.append(jnp.where(spread[None] == place, one, zero).reshape(HALF, BLOCK))
            left = jnp.concatenate(lefts, axis=0).astype(jnp.bfloat16)
            hot = jnp.concatenate(hots, axis=0)
            moved = lax.dot_general(left, hot, NT, preferred_element_type=jnp.float32)
            for side in range(2):
                p = 2 * pair + side
                row = p // per * rows + p % per
                part = moved[8 * side : 8 * side + 8, HALF * side : HALF * side + HALF]
                shuf_a[pl.ds(row, 3, stride=per), :] = part[0:3]
                shuf_b[pl.ds(row, 3, stride=per), :] = part[4:7]
        designs[:, at] = jnp.concatenate([shuf_a[...], shuf_b[...]], axis=1).astype(jnp.bfloat16)

        load(b).wait()
        cells = pl.ds(pl.multiple_of(b * span, span), span)
        flat[cells, :] = raw[cells, :].astype(jnp.float32)
        return carry

    lax.fori_loop(0, blocks, shuffle, 0)

    crossed = lax.dot_general(designs[...], des_all[...], NT, preferred_element_type=jnp.float32)
    for g in range(n):
        out_x[g, 0:rows, 0:16] = crossed[g * rows : (g + 1) * rows]
        out_x[g, rows:, 0:16] = crossed[top : top + 8]

    pl.semaphore_wait(barrier, n + m - 2)

    def exchange(src, dst, send_sem, recv_sem):
        made = []
        for o in range(1, n):
            to = lax.rem(me + o, n)
            made.append(pltpu.make_async_remote_copy(
                src_ref=src(to), dst_ref=dst(o), send_sem=send_sem(o), recv_sem=recv_sem(o),
                device_id=(to, slab), device_id_type=MESH))
            made[-1].start()
        return made

    copies_x = exchange(
        lambda g: out_x.at[g], lambda o: got_x.at[o], lambda o: xsend.at[o], lambda o: xrecv.at[o])
    got_x[0] = out_x[me]

    group = min(4, blocks)
    depth_k = group * BLOCK
    sub = lax.broadcasted_iota(jnp.int32, (8, wide), 0)
    per_slice = tiles // 2
    copies_t = []
    for tile in range(tiles):
        first_row = [2 * (2 * (tile % per_slice) + i) + tile // per_slice for i in range(2)]

        def multiply(k, carry):
            acc, sq = carry
            start = pl.multiple_of(k * depth_k * flat_rows, depth_k * flat_rows)
            part = jnp.concatenate(
                [flat[pl.ds(start + r, depth_k, stride=flat_rows), :] for r in first_row], axis=1)
            at = pl.ds(pl.multiple_of(k * depth_k, depth_k), depth_k)
            acc = acc + jnp.dot(
                designs[:, at], part.astype(jnp.bfloat16), preferred_element_type=jnp.float32)
            sq = sq + jnp.sum((part * part).reshape(depth_k // 8, 8, wide), axis=0)
            return acc, sq

        acc, sq = lax.fori_loop(
            0, blocks // group, multiply,
            (jnp.zeros((designs.shape[0], wide), jnp.float32), jnp.zeros((8, wide), jnp.float32)))
        squares = jnp.sum(sq, axis=0, keepdims=True)
        seen_rows = jnp.where(sub == 4, squares, acc[top : top + 8])
        for g in range(n):
            out[tile, g, 0:rows, :] = acc[g * rows : (g + 1) * rows]
            out[tile, g, rows:, :] = seen_rows
        copies_t.append(exchange(
            lambda g: out.at[tile, g], lambda o: got.at[tile, o],
            lambda o: send.at[tile, o], lambda o: recv.at[tile, o]))
        got[tile, 0] = out[tile, me]

    cells = mask_ref[...].astype(jnp.float32)
    mask_row = jnp.concatenate([cells[0:1], cells[1:2]], axis=1)

    def source(s):
        return lax.rem(me - s + n, n)

    for copy in copies_x:
        copy.wait()
    seen_x = got_x[source(0), rows:]
    for s in range(1, n):
        seen_x = seen_x + got_x[source(s), rows:]
    mine_x = got_x[0, 0:rows]
    for o in range(1, n):
        mine_x = mine_x + got_x[o, 0:rows]
    gram = [[seen_x[i : i + 1, j : j + 1] for j in range(4)] for i in range(4)]
    low_z = cholesky([row[1:4] for row in gram[1:4]])
    inv_z = [1.0 / low_z[i][i] for i in range(3)]
    low_f = cholesky(gram)
    inv_diag = [1.0 / low_f[i][i] for i in range(4)]
    unit = [jnp.zeros((1, 1), jnp.float32), jnp.ones((1, 1), jnp.float32)]
    columns = [cho_solve(low_f, inv_diag, [unit[int(i == j)] for i in range(4)]) for j in range(4)]
    inverse = [[columns[j][i] for j in range(4)] for i in range(4)]

    for tile in range(tiles):
        for copy in copies_t[tile]:
            copy.wait()
        cols = slice(tile * wide, (tile + 1) * wide)
        obs = got[tile, source(0), rows:]
        for s in range(1, n):
            obs = obs + got[tile, source(s), rows:]
        chunk = got[tile, 0, 0:rows]
        for o in range(1, n):
            chunk = chunk + got[tile, o, 0:rows]
        prod = [obs[k : k + 1] for k in range(4)]
        fit = cho_solve(low_z, inv_z, prod[1:4])
        resid = obs[4:5] - (prod[1] * fit[0] + prod[2] * fit[1] + prod[3] * fit[2])

        def statistic(proj):
            slope = sum(inverse[0][k] * proj[k] for k in range(4))
            quad = sum(proj[k] * sum(inverse[k][l] * proj[l] for l in range(4)) for k in range(4))
            return slope / jnp.sqrt((resid - quad) / freedom * inverse[0][0])

        seen = [prod[k] - sum(gram[k][1 + i] * fit[i] for i in range(3)) for k in range(4)]
        own_o[:, cols] = statistic(seen) * mask_row[:, cols]
        proj = []
        for c in range(3):
            at = slice(c * per, (c + 1) * per)
            proj.append(chunk[at] - sum(mine_x[at, 1 + i : 2 + i] * fit[i] for i in range(3)))
        own[:, cols] = statistic([proj[0], seen[1], proj[1], proj[2]]) * mask_row[:, cols]

    up = (me, lax.rem(slab + 1, m))
    down = (me, lax.rem(slab + m - 1, m))

    def halo(src, dst, k, to):
        return pltpu.make_async_remote_copy(
            src_ref=src, dst_ref=dst, send_sem=hsend.at[k], recv_sem=hrecv.at[k],
            device_id=to, device_id_type=MESH)

    rise = [halo(own, low, 0, up), halo(own_o, low_o, 1, up)]
    fall = [halo(own, high, 2, down), halo(own_o, high_o, 3, down)]

    @pl.when(slab < m - 1)
    def _():
        for copy in rise:
            copy.start()

    @pl.when(slab > 0)
    def _():
        for copy in fall:
            copy.start()

    @pl.when(slab == 0)
    def _():
        low[...] = jnp.zeros_like(low)
        low_o[...] = jnp.zeros_like(low_o)

    @pl.when(slab == m - 1)
    def _():
        high[...] = jnp.zeros_like(high)
        high_o[...] = jnp.zeros_like(high_o)

    field[...] = jnp.zeros_like(field)

    @pl.when(slab > 0)
    def _():
        for copy in rise:
            copy.wait_recv()

    @pl.when(slab < m - 1)
    def _():
        for copy in fall:
            copy.wait_recv()

    def deep(lower, mine, upper):
        slices = []
        for ref in (lower, mine, upper):
            value = ref[...]
            slices += [value[:, :plane], value[:, plane:]]
        return [
            sum(gauss_taps[position] * slices[position + z] for position in range(5))
            for z in range(2)
        ]

    first, second = deep(low, own, high)
    field[0:per, :] = first
    field[8 : 8 + per, :] = second
    first, second = deep(low_o, own_o, high_o)
    field[16:17, :] = first
    field[17:18, :] = second

    cell = lax.broadcasted_iota(jnp.int32, (24, plane), 1)
    smooth = blur(field[...], PY, cell // PY, PX)
    smooth = blur(smooth, 1, cell % PY, PY)

    peaks = jnp.maximum(
        jnp.max(jnp.where(cells[0:1] > 0, smooth[0:per] * cells[0:1], -1e30), axis=1, keepdims=True),
        jnp.max(jnp.where(cells[1:2] > 0, smooth[8 : 8 + per] * cells[1:2], -1e30), axis=1, keepdims=True),
    )
    pk1[0] = jnp.broadcast_to(peaks, (per, LANES))
    copies_p = []
    for o in range(1, m):
        copies_p.append(pltpu.make_async_remote_copy(
            src_ref=pk1.at[0], dst_ref=pk1.at[o], send_sem=psend.at[o], recv_sem=prec.at[o],
            device_id=(me, lax.rem(slab + o, m)), device_id_type=MESH))
        copies_p[-1].start()
    seen_t = [smooth[16 + z : 17 + z] * cells[z : z + 1] for z in range(2)]
    smooth_ref[...] = jnp.concatenate(seen_t, axis=0)

    for copy in copies_p:
        copy.wait_recv()
    best = pk1[0]
    for o in range(1, m):
        best = jnp.maximum(best, pk1[o])
    pk2[0] = best
    copies_q = []
    for o in range(1, n):
        copies_q.append(pltpu.make_async_remote_copy(
            src_ref=pk2.at[0], dst_ref=pk2.at[o], send_sem=qsend.at[o], recv_sem=qrec.at[o],
            device_id=(lax.rem(me + o, n), slab), device_id_type=MESH))
        copies_q[-1].start()
    for copy in copies_q:
        copy.wait_recv()

    for o in range(n):
        peak_ref[lax.rem(me - o + n, n)] = pk2[o]

    for copy in copies_p + copies_q:
        copy.wait_send()

    @pl.when(slab < m - 1)
    def _():
        for copy in rise:
            copy.wait_send()

    @pl.when(slab > 0)
    def _():
        for copy in fall:
            copy.wait_send()


def p_kernel(smooth_ref, peaks_ref, mask_ref, t_ref, pval_ref, line_ref):
    n, per = peaks_ref.shape[:2]
    copies = n * per
    cells = mask_ref[...].astype(jnp.float32)
    values = smooth_ref[...]
    t_ref[...] = values
    line = jnp.zeros((1, LANES), jnp.float32)
    sub = lax.broadcasted_iota(jnp.int32, (per, LANES), 0)
    lane = lax.broadcasted_iota(jnp.int32, (per, LANES), 1)
    counts = [jnp.zeros((1, values.shape[1]), jnp.float32) for _ in range(2)]
    for d in range(n):
        value = peaks_ref[d]
        line = line + jnp.sum(jnp.where(lane == sub + d * per, value, 0.0), axis=0, keepdims=True)
        for z in range(2):
            level = jax.nn.sigmoid((value[:, 0:1] - values[z : z + 1]) / 0.2)
            counts[z] = counts[z] + jnp.sum(level, axis=0, keepdims=True)
    pval_ref[...] = cells * (1.0 + jnp.concatenate(counts, axis=0)) / (copies + 1)
    line_ref[...] = line[:, :copies]


def body(n, m, subjects_data, covariates, permutes, brain_mask):
    subj_rows, depth, plane = subjects_data.shape
    assert depth == 2 and plane == PX * PY
    copies = permutes.shape[0]
    per = copies // n
    rows = -(-3 * per // 8) * 8
    voxels = depth * plane
    wide = 2 * LANES
    tiles = voxels // wide
    lane_tiles = plane // LANES
    flat_rows = depth * lane_tiles
    data = (
        subjects_data.reshape(subj_rows, depth, lane_tiles, LANES)
        .transpose(0, 2, 1, 3)
        .reshape(subj_rows * flat_rows, LANES)
    )
    height = -(-(n * rows + 8) // 16) * 16
    f32 = jnp.float32
    bf16 = jnp.bfloat16
    vmem = pl.BlockSpec(memory_space=pltpu.VMEM)
    anywhere = pl.BlockSpec(memory_space=pl.ANY)
    dma = pltpu.SemaphoreType.DMA
    smooth, peaks = pl.pallas_call(
        functools.partial(maps_kernel, n, m, per, float(n * subj_rows - 4)),
        in_specs=[anywhere] * 4,
        out_specs=[vmem] * 2,
        out_shape=[
            jax.ShapeDtypeStruct((depth, plane), f32),
            jax.ShapeDtypeStruct((n, per, LANES), f32),
        ],
        scratch_shapes=[
            pltpu.VMEM((subj_rows * flat_rows, LANES), bf16),
            pltpu.VMEM((3, subj_rows), bf16),
            pltpu.VMEM((copies, subj_rows), jnp.int32),
            pltpu.VMEM((depth, plane), jnp.int32),
            pltpu.VMEM((subj_rows * flat_rows, LANES), f32),
            pltpu.VMEM((height, HALF), f32),
            pltpu.VMEM((height, HALF), f32),
            pltpu.VMEM((24, BLOCK), f32),
            pltpu.VMEM((16, subj_rows), bf16),
            pltpu.VMEM((height, subj_rows), bf16),
            pltpu.VMEM((n, rows + 8, LANES), f32),
            pltpu.VMEM((n, rows + 8, LANES), f32),
            pltpu.VMEM((tiles, n, rows + 8, wide), f32),
            pltpu.VMEM((tiles, n, rows + 8, wide), f32),
            pltpu.VMEM((per, voxels), f32),
            pltpu.VMEM((1, voxels), f32),
            pltpu.VMEM((per, voxels), f32),
            pltpu.VMEM((1, voxels), f32),
            pltpu.VMEM((per, voxels), f32),
            pltpu.VMEM((1, voxels), f32),
            pltpu.VMEM((24, plane), f32),
            pltpu.VMEM((m, per, LANES), f32),
            pltpu.VMEM((n, per, LANES), f32),
            dma((subj_rows // BLOCK,)), dma((3,)), dma((n,)), dma((n,)),
            dma((tiles, n)), dma((tiles, n)),
            dma((4,)), dma((4,)), dma((m,)), dma((m,)), dma((n,)), dma((n,)),
        ],
        compiler_params=pltpu.CompilerParams(
            collective_id=0, has_side_effects=True, vmem_limit_bytes=60 * 2**20
        ),
        name="maps",
    )(data, covariates, permutes, brain_mask)
    smooth_t, p_values, line = pl.pallas_call(
        p_kernel,
        in_specs=[vmem] * 3,
        out_specs=[vmem] * 3,
        out_shape=[
            jax.ShapeDtypeStruct((depth, plane), f32),
            jax.ShapeDtypeStruct((depth, plane), f32),
            jax.ShapeDtypeStruct((1, copies), f32),
        ],
        name="p_values",
    )(smooth, peaks, brain_mask)
    return smooth_t, p_values, line.reshape(copies)


def solution(mesh):
    return jax.shard_map(
        functools.partial(body, mesh.shape["subj"], mesh.shape["slab"]),
        mesh=mesh,
        in_specs=(P("subj", "slab", None), P(None, "subj"), P(None, "subj"), P("slab", None)),
        out_specs=(P("slab", None), P("slab", None), P()),
        check_vma=False,
    )
```

```python
import functools
import math

import jax
import jax.numpy as jnp
from jax import lax
from jax.experimental import pallas as pl
from jax.experimental.pallas import tpu as pltpu
from jax.sharding import PartitionSpec as P

BLOCK = 256
HALF = 128
QUARTER = 64
PX = 16
PY = 32
LANES = 128
MESH = pl.DeviceIdType.MESH

gauss_raw = tuple((math.exp(-0.5 * (offset - 2) ** 2) for offset in range(5)))
gauss_taps = tuple((value / sum(gauss_raw) for value in gauss_raw))

NT = (((1,), (1,)), ((), ()))


def cholesky(mat):
    size = len(mat)
    low = [[None] * size for _ in range(size)]
    for j in range(size):
        total = mat[j][j]
        for k in range(j):
            total = total - low[j][k] * low[j][k]
        low[j][j] = jnp.sqrt(total)
        for i in range(j + 1, size):
            total = mat[i][j]
            for k in range(j):
                total = total - low[i][k] * low[j][k]
            low[i][j] = total / low[j][j]
    return low


def cho_solve(low, inv_diag, rhs):
    size = len(low)
    half = []
    for i in range(size):
        total = rhs[i]
        for k in range(i):
            total = total - low[i][k] * half[k]
        half.append(total * inv_diag[i])
    out = [None] * size
    for i in reversed(range(size)):
        total = half[i]
        for k in range(i + 1, size):
            total = total - low[k][i] * out[k]
        out[i] = total * inv_diag[i]
    return out


def blur(cells, stride, coord, size):
    width = cells.shape[1]
    total = None
    for position in range(5):
        d = position - 2
        moved = cells if d == 0 else pltpu.roll(cells, (-d * stride) % width, 1)
        inside = (coord + d >= 0) & (coord + d < size)
        term = gauss_taps[position] * jnp.where(inside, moved, 0.0)
        total = term if total is None else total + term
    return total


def maps_kernel(
    n, m, per, freedom,
    x_hbm, cov_hbm, perm_hbm, mask_hbm, smooth_ref, peak_ref,
    raw, cov_ref, perm_ref, mask_ref, flat, shuf_a, shuf_b, des, des_all, designs,
    out_x, got_x, out, got, own, own_o, low, low_o, high, high_o, field, pk1, pk2,
    xsem, csem, xsend, xrecv, send, recv, hsend, hrecv, psend, prec, qsend, qrec,
):
    me = lax.axis_index("subj")
    slab = lax.axis_index("slab")
    plane = mask_ref.shape[1]
    copies = perm_ref.shape[0]
    rows = out.shape[2] - 8
    top = n * rows
    wide = out.shape[3]
    tiles = out.shape[0]
    blocks = perm_ref.shape[1] // BLOCK
    flat_rows = raw.shape[0] // perm_ref.shape[1]
    span = BLOCK * flat_rows

    small = [
        pltpu.make_async_copy(src, dst, csem.at[i])
        for i, (src, dst) in enumerate(((perm_hbm, perm_ref), (cov_hbm, cov_ref), (mask_hbm, mask_ref)))
    ]
    for copy in small:
        copy.start()

    def load(b):
        at = pl.ds(pl.multiple_of(b * span, span), span)
        return pltpu.make_async_copy(x_hbm.at[at], raw.at[at], xsem.at[b])

    def start_load(b, carry):
        load(b).start()
        return carry

    lax.fori_loop(0, blocks, start_load, 0)

    barrier = pltpu.get_barrier_semaphore()
    for o in range(1, n):
        pl.semaphore_signal(barrier, inc=1, device_id=(lax.rem(me + o, n), slab), device_id_type=MESH)
    for o in range(1, m):
        pl.semaphore_signal(barrier, inc=1, device_id=(me, lax.rem(slab + o, m)), device_id_type=MESH)

    shuf_a[...] = jnp.zeros_like(shuf_a)
    shuf_b[...] = jnp.zeros_like(shuf_b)
    des[...] = jnp.zeros_like(des)
    out_x[...] = jnp.zeros_like(out_x)
    for copy in small:
        copy.wait()

    row_high = lax.broadcasted_iota(jnp.int32, (16, BLOCK), 0) // 4
    left_half = lax.broadcasted_iota(jnp.int32, (4, HALF), 1) < QUARTER
    one = jnp.ones((), jnp.bfloat16)
    zero = jnp.zeros((), jnp.bfloat16)

    def shuffle(b, carry):
        at = pl.ds(pl.multiple_of(b * BLOCK, BLOCK), BLOCK)
        place = (
            lax.broadcasted_iota(jnp.int32, (QUARTER // 16, 16, BLOCK), 0) * 16
            + lax.broadcasted_iota(jnp.int32, (QUARTER // 16, 16, BLOCK), 1)
        ).astype(jnp.float32).astype(jnp.bfloat16)
        cov = cov_ref[:, at].astype(jnp.float32)
        for i in range(4):
            des[4 * i : 4 * i + 3, :] = cov
        des[16:17, :] = cov[0:1]
        des[17:18, :] = jnp.ones((1, BLOCK), jnp.float32)
        des[18:20, :] = cov[1:3]
        shuf_a[top : top + 4, :] = des[16:20, 0:HALF]
        shuf_b[top : top + 4, :] = des[16:20, HALF:BLOCK]
        des_all[:, at] = des[16:32, :].astype(jnp.bfloat16)

        local = perm_ref[:, at] & (BLOCK - 1)
        upper = local // QUARTER
        lower = (local & (QUARTER - 1)).astype(jnp.float32)
        base = des[0:16, :]
        for quad in range(copies // 4):
            lefts = []
            hots = []
            for p in range(4 * quad, 4 * quad + 4):
                lefts.append(jnp.where(upper[p : p + 1] == row_high, base, 0.0).astype(jnp.bfloat16))
                spread = jnp.broadcast_to(lower[p : p + 1], (16, BLOCK)).astype(jnp.bfloat16)
                hots.append(jnp.where(spread[None] == place, one, zero).reshape(QUARTER, BLOCK))
            left = jnp.concatenate(lefts, axis=0)
            hot = jnp.concatenate(hots, axis=0)
            moved = lax.dot_general(left, hot, NT, preferred_element_type=jnp.float32)
            for side in range(4):
                p = 4 * quad + side
                row = p // per * rows + p % per
                tile_lanes = slice(HALF * (side // 2), HALF * (side // 2) + HALF)
                for half, shuf in enumerate((shuf_a, shuf_b)):
                    first = 16 * side + 8 * half
                    part = moved[first : first + 8, tile_lanes]
                    turned = pltpu.roll(part, QUARTER, 1)
                    if side % 2 == 0:
                        joined = jnp.where(left_half, part[0:4], turned[4:8])
                    else:
                        joined = jnp.where(left_half, turned[0:4], part[4:8])
                    shuf[pl.ds(row, 3, stride=per), :] = joined[0:3]
        designs[:, at] = jnp.concatenate([shuf_a[...], shuf_b[...]], axis=1).astype(jnp.bfloat16)

        load(b).wait()
        cells = pl.ds(pl.multiple_of(b * span, span), span)
        flat[cells, :] = raw[cells, :].astype(jnp.float32)
        return carry

    lax.fori_loop(0, blocks, shuffle, 0)

    crossed = lax.dot_general(designs[...], des_all[...], NT, preferred_element_type=jnp.float32)
    for g in range(n):
        out_x[g, 0:rows, 0:16] = crossed[g * rows : (g + 1) * rows]
        out_x[g, rows:, 0:16] = crossed[top : top + 8]

    pl.semaphore_wait(barrier, n + m - 2)

    def exchange(src, dst, send_sem, recv_sem):
        made = []
        for o in range(1, n):
            to = lax.rem(me + o, n)
            made.append(pltpu.make_async_remote_copy(
                src_ref=src(to), dst_ref=dst(o), send_sem=send_sem(o), recv_sem=recv_sem(o),
                device_id=(to, slab), device_id_type=MESH))
            made[-1].start()
        return made

    copies_x = exchange(
        lambda g: out_x.at[g], lambda o: got_x.at[o], lambda o: xsend.at[o], lambda o: xrecv.at[o])
    got_x[0] = out_x[me]

    group = min(4, blocks)
    depth_k = group * BLOCK
    sub = lax.broadcasted_iota(jnp.int32, (8, wide), 0)
    per_slice = tiles // 2
    copies_t = []
    for tile in range(tiles):
        first_row = [2 * (2 * (tile % per_slice) + i) + tile // per_slice for i in range(2)]

        def multiply(k, carry):
            acc, sq = carry
            start = pl.multiple_of(k * depth_k * flat_rows, depth_k * flat_rows)
            part = jnp.concatenate(
                [flat[pl.ds(start + r, depth_k, stride=flat_rows), :] for r in first_row], axis=1)
            at = pl.ds(pl.multiple_of(k * depth_k, depth_k), depth_k)
            acc = acc + jnp.dot(
                designs[:, at], part.astype(jnp.bfloat16), preferred_element_type=jnp.float32)
            sq = sq + jnp.sum((part * part).reshape(depth_k // 8, 8, wide), axis=0)
            return acc, sq

        acc, sq = lax.fori_loop(
            0, blocks // group, multiply,
            (jnp.zeros((designs.shape[0], wide), jnp.float32), jnp.zeros((8, wide), jnp.float32)))
        squares = jnp.sum(sq, axis=0, keepdims=True)
        seen_rows = jnp.where(sub == 4, squares, acc[top : top + 8])
        for g in range(n):
            out[tile, g, 0:rows, :] = acc[g * rows : (g + 1) * rows]
            out[tile, g, rows:, :] = seen_rows
        copies_t.append(exchange(
            lambda g: out.at[tile, g], lambda o: got.at[tile, o],
            lambda o: send.at[tile, o], lambda o: recv.at[tile, o]))
        got[tile, 0] = out[tile, me]

    cells = mask_ref[...].astype(jnp.float32)
    mask_row = jnp.concatenate([cells[0:1], cells[1:2]], axis=1)

    def source(s):
        return lax.rem(me - s + n, n)

    for copy in copies_x:
        copy.wait()
    seen_x = got_x[source(0), rows:]
    for s in range(1, n):
        seen_x = seen_x + got_x[source(s), rows:]
    mine_x = got_x[0, 0:rows]
    for o in range(1, n):
        mine_x = mine_x + got_x[o, 0:rows]
    gram = [[seen_x[i : i + 1, j : j + 1] for j in range(4)] for i in range(4)]
    low_z = cholesky([row[1:4] for row in gram[1:4]])
    inv_z = [1.0 / low_z[i][i] for i in range(3)]
    low_f = cholesky(gram)
    inv_diag = [1.0 / low_f[i][i] for i in range(4)]
    unit = [jnp.zeros((1, 1), jnp.float32), jnp.ones((1, 1), jnp.float32)]
    columns = [cho_solve(low_f, inv_diag, [unit[int(i == j)] for i in range(4)]) for j in range(4)]
    inverse = [[columns[j][i] for j in range(4)] for i in range(4)]

    for tile in range(tiles):
        for copy in copies_t[tile]:
            copy.wait()
        cols = slice(tile * wide, (tile + 1) * wide)
        obs = got[tile, source(0), rows:]
        for s in range(1, n):
            obs = obs + got[tile, source(s), rows:]
        chunk = got[tile, 0, 0:rows]
        for o in range(1, n):
            chunk = chunk + got[tile, o, 0:rows]
        prod = [obs[k : k + 1] for k in range(4)]
        fit = cho_solve(low_z, inv_z, prod[1:4])
        resid = obs[4:5] - (prod[1] * fit[0] + prod[2] * fit[1] + prod[3] * fit[2])

        def statistic(proj):
            slope = sum(inverse[0][k] * proj[k] for k in range(4))
            quad = sum(proj[k] * sum(inverse[k][l] * proj[l] for l in range(4)) for k in range(4))
            return slope / jnp.sqrt((resid - quad) / freedom * inverse[0][0])

        seen = [prod[k] - sum(gram[k][1 + i] * fit[i] for i in range(3)) for k in range(4)]
        own_o[:, cols] = statistic(seen) * mask_row[:, cols]
        proj = []
        for c in range(3):
            at = slice(c * per, (c + 1) * per)
            proj.append(chunk[at] - sum(mine_x[at, 1 + i : 2 + i] * fit[i] for i in range(3)))
        own[:, cols] = statistic([proj[0], seen[1], proj[1], proj[2]]) * mask_row[:, cols]

    up = (me, lax.rem(slab + 1, m))
    down = (me, lax.rem(slab + m - 1, m))

    def halo(src, dst, k, to):
        return pltpu.make_async_remote_copy(
            src_ref=src, dst_ref=dst, send_sem=hsend.at[k], recv_sem=hrecv.at[k],
            device_id=to, device_id_type=MESH)

    rise = [halo(own, low, 0, up), halo(own_o, low_o, 1, up)]
    fall = [halo(own, high, 2, down), halo(own_o, high_o, 3, down)]

    @pl.when(slab < m - 1)
    def _():
        for copy in rise:
            copy.start()

    @pl.when(slab > 0)
    def _():
        for copy in fall:
            copy.start()

    @pl.when(slab == 0)
    def _():
        low[...] = jnp.zeros_like(low)
        low_o[...] = jnp.zeros_like(low_o)

    @pl.when(slab == m - 1)
    def _():
        high[...] = jnp.zeros_like(high)
        high_o[...] = jnp.zeros_like(high_o)

    field[...] = jnp.zeros_like(field)

    @pl.when(slab > 0)
    def _():
        for copy in rise:
            copy.wait_recv()

    @pl.when(slab < m - 1)
    def _():
        for copy in fall:
            copy.wait_recv()

    def deep(lower, mine, upper):
        slices = []
        for ref in (lower, mine, upper):
            value = ref[...]
            slices += [value[:, :plane], value[:, plane:]]
        return [
            sum(gauss_taps[position] * slices[position + z] for position in range(5))
            for z in range(2)
        ]

    first, second = deep(low, own, high)
    field[0:per, :] = first
    field[8 : 8 + per, :] = second
    first, second = deep(low_o, own_o, high_o)
    field[16:17, :] = first
    field[17:18, :] = second

    cell = lax.broadcasted_iota(jnp.int32, (24, plane), 1)
    smooth = blur(field[...], PY, cell // PY, PX)
    smooth = blur(smooth, 1, cell % PY, PY)

    peaks = jnp.maximum(
        jnp.max(jnp.where(cells[0:1] > 0, smooth[0:per] * cells[0:1], -1e30), axis=1, keepdims=True),
        jnp.max(jnp.where(cells[1:2] > 0, smooth[8 : 8 + per] * cells[1:2], -1e30), axis=1, keepdims=True),
    )
    pk1[0] = jnp.broadcast_to(peaks, (per, LANES))
    copies_p = []
    for o in range(1, m):
        copies_p.append(pltpu.make_async_remote_copy(
            src_ref=pk1.at[0], dst_ref=pk1.at[o], send_sem=psend.at[o], recv_sem=prec.at[o],
            device_id=(me, lax.rem(slab + o, m)), device_id_type=MESH))
        copies_p[-1].start()
    seen_t = [smooth[16 + z : 17 + z] * cells[z : z + 1] for z in range(2)]
    smooth_ref[...] = jnp.concatenate(seen_t, axis=0)

    for copy in copies_p:
        copy.wait_recv()
    best = pk1[0]
    for o in range(1, m):
        best = jnp.maximum(best, pk1[o])
    pk2[0] = best
    copies_q = []
    for o in range(1, n):
        copies_q.append(pltpu.make_async_remote_copy(
            src_ref=pk2.at[0], dst_ref=pk2.at[o], send_sem=qsend.at[o], recv_sem=qrec.at[o],
            device_id=(lax.rem(me + o, n), slab), device_id_type=MESH))
        copies_q[-1].start()
    for copy in copies_q:
        copy.wait_recv()

    for o in range(n):
        peak_ref[lax.rem(me - o + n, n)] = pk2[o]

    for copy in copies_p + copies_q:
        copy.wait_send()

    @pl.when(slab < m - 1)
    def _():
        for copy in rise:
            copy.wait_send()

    @pl.when(slab > 0)
    def _():
        for copy in fall:
            copy.wait_send()


def p_kernel(smooth_ref, peaks_ref, mask_ref, t_ref, pval_ref, line_ref):
    n, per = peaks_ref.shape[:2]
    copies = n * per
    cells = mask_ref[...].astype(jnp.float32)
    values = smooth_ref[...]
    t_ref[...] = values
    line = jnp.zeros((1, LANES), jnp.float32)
    sub = lax.broadcasted_iota(jnp.int32, (per, LANES), 0)
    lane = lax.broadcasted_iota(jnp.int32, (per, LANES), 1)
    counts = [jnp.zeros((1, values.shape[1]), jnp.float32) for _ in range(2)]
    for d in range(n):
        value = peaks_ref[d]
        line = line + jnp.sum(jnp.where(lane == sub + d * per, value, 0.0), axis=0, keepdims=True)
        for z in range(2):
            level = jax.nn.sigmoid((value[:, 0:1] - values[z : z + 1]) / 0.2)
            counts[z] = counts[z] + jnp.sum(level, axis=0, keepdims=True)
    pval_ref[...] = cells * (1.0 + jnp.concatenate(counts, axis=0)) / (copies + 1)
    line_ref[...] = line[:, :copies]


def body(n, m, subjects_data, covariates, permutes, brain_mask):
    subj_rows, depth, plane = subjects_data.shape
    assert depth == 2 and plane == PX * PY
    copies = permutes.shape[0]
    per = copies // n
    rows = -(-3 * per // 8) * 8
    voxels = depth * plane
    wide = 2 * LANES
    tiles = voxels // wide
    lane_tiles = plane // LANES
    flat_rows = depth * lane_tiles
    data = (
        subjects_data.reshape(subj_rows, depth, lane_tiles, LANES)
        .transpose(0, 2, 1, 3)
        .reshape(subj_rows * flat_rows, LANES)
    )
    height = -(-(n * rows + 8) // 16) * 16
    f32 = jnp.float32
    bf16 = jnp.bfloat16
    vmem = pl.BlockSpec(memory_space=pltpu.VMEM)
    anywhere = pl.BlockSpec(memory_space=pl.ANY)
    dma = pltpu.SemaphoreType.DMA
    smooth, peaks = pl.pallas_call(
        functools.partial(maps_kernel, n, m, per, float(n * subj_rows - 4)),
        in_specs=[anywhere] * 4,
        out_specs=[vmem] * 2,
        out_shape=[
            jax.ShapeDtypeStruct((depth, plane), f32),
            jax.ShapeDtypeStruct((n, per, LANES), f32),
        ],
        scratch_shapes=[
            pltpu.VMEM((subj_rows * flat_rows, LANES), bf16),
            pltpu.VMEM((3, subj_rows), bf16),
            pltpu.VMEM((copies, subj_rows), jnp.int32),
            pltpu.VMEM((depth, plane), jnp.int32),
            pltpu.VMEM((subj_rows * flat_rows, LANES), f32),
            pltpu.VMEM((height, HALF), f32),
            pltpu.VMEM((height, HALF), f32),
            pltpu.VMEM((32, BLOCK), f32),
            pltpu.VMEM((16, subj_rows), bf16),
            pltpu.VMEM((height, subj_rows), bf16),
            pltpu.VMEM((n, rows + 8, LANES), f32),
            pltpu.VMEM((n, rows + 8, LANES), f32),
            pltpu.VMEM((tiles, n, rows + 8, wide), f32),
            pltpu.VMEM((tiles, n, rows + 8, wide), f32),
            pltpu.VMEM((per, voxels), f32),
            pltpu.VMEM((1, voxels), f32),
            pltpu.VMEM((per, voxels), f32),
            pltpu.VMEM((1, voxels), f32),
            pltpu.VMEM((per, voxels), f32),
            pltpu.VMEM((1, voxels), f32),
            pltpu.VMEM((24, plane), f32),
            pltpu.VMEM((m, per, LANES), f32),
            pltpu.VMEM((n, per, LANES), f32),
            dma((subj_rows // BLOCK,)), dma((3,)), dma((n,)), dma((n,)),
            dma((tiles, n)), dma((tiles, n)),
            dma((4,)), dma((4,)), dma((m,)), dma((m,)), dma((n,)), dma((n,)),
        ],
        compiler_params=pltpu.CompilerParams(
            collective_id=0, has_side_effects=True, vmem_limit_bytes=60 * 2**20
        ),
        name="maps",
    )(data, covariates, permutes, brain_mask)
    smooth_t, p_values, line = pl.pallas_call(
        p_kernel,
        in_specs=[vmem] * 3,
        out_specs=[vmem] * 3,
        out_shape=[
            jax.ShapeDtypeStruct((depth, plane), f32),
            jax.ShapeDtypeStruct((depth, plane), f32),
            jax.ShapeDtypeStruct((1, copies), f32),
        ],
        name="p_values",
    )(smooth, peaks, brain_mask)
    return smooth_t, p_values, line.reshape(copies)


def solution(mesh):
    return jax.shard_map(
        functools.partial(body, mesh.shape["subj"], mesh.shape["slab"]),
        mesh=mesh,
        in_specs=(P("subj", "slab", None), P(None, "subj"), P(None, "subj"), P("slab", None)),
        out_specs=(P("slab", None), P("slab", None), P()),
        check_vma=False,
    )
```

```python
import functools
import math

import jax
import jax.numpy as jnp
from jax import lax
from jax.experimental import pallas as pl
from jax.experimental.pallas import tpu as pltpu
from jax.sharding import PartitionSpec as P

BLOCK = 256
HALF = 128
QUARTER = 64
PX = 16
PY = 32
LANES = 128
MESH = pl.DeviceIdType.MESH

gauss_raw = tuple((math.exp(-0.5 * (offset - 2) ** 2) for offset in range(5)))
gauss_taps = tuple((value / sum(gauss_raw) for value in gauss_raw))

NT = (((1,), (1,)), ((), ()))


def cholesky(mat):
    size = len(mat)
    low = [[None] * size for _ in range(size)]
    for j in range(size):
        total = mat[j][j]
        for k in range(j):
            total = total - low[j][k] * low[j][k]
        low[j][j] = jnp.sqrt(total)
        for i in range(j + 1, size):
            total = mat[i][j]
            for k in range(j):
                total = total - low[i][k] * low[j][k]
            low[i][j] = total / low[j][j]
    return low


def cho_solve(low, inv_diag, rhs):
    size = len(low)
    half = []
    for i in range(size):
        total = rhs[i]
        for k in range(i):
            total = total - low[i][k] * half[k]
        half.append(total * inv_diag[i])
    out = [None] * size
    for i in reversed(range(size)):
        total = half[i]
        for k in range(i + 1, size):
            total = total - low[k][i] * out[k]
        out[i] = total * inv_diag[i]
    return out


def blur(cells, stride, coord, size):
    width = cells.shape[1]
    total = None
    for position in range(5):
        d = position - 2
        moved = cells if d == 0 else pltpu.roll(cells, (-d * stride) % width, 1)
        inside = (coord + d >= 0) & (coord + d < size)
        term = gauss_taps[position] * jnp.where(inside, moved, 0.0)
        total = term if total is None else total + term
    return total


def maps_kernel(
    n, m, per, freedom,
    x_hbm, cov_hbm, perm_hbm, mask_hbm, smooth_ref, peak_ref,
    raw, cov_ref, perm_ref, mask_ref, flat, shuf_a, shuf_b, des, des_all, designs,
    out_x, got_x, out, got, own, own_o, low, low_o, high, high_o, field, pk1,
    xsem, csem, xsend, xrecv, send, recv, hsend, hrecv, psend, prec,
):
    me = lax.axis_index("subj")
    slab = lax.axis_index("slab")
    plane = mask_ref.shape[1]
    copies = perm_ref.shape[0]
    rows = out.shape[2] - 8
    top = n * rows
    wide = out.shape[3]
    tiles = out.shape[0]
    blocks = perm_ref.shape[1] // BLOCK
    flat_rows = raw.shape[0] // perm_ref.shape[1]
    span = BLOCK * flat_rows

    small = [
        pltpu.make_async_copy(src, dst, csem.at[i])
        for i, (src, dst) in enumerate(((perm_hbm, perm_ref), (cov_hbm, cov_ref), (mask_hbm, mask_ref)))
    ]
    for copy in small:
        copy.start()

    def load(b):
        at = pl.ds(pl.multiple_of(b * span, span), span)
        return pltpu.make_async_copy(x_hbm.at[at], raw.at[at], xsem.at[b])

    def start_load(b, carry):
        load(b).start()
        return carry

    lax.fori_loop(0, blocks, start_load, 0)

    barrier = pltpu.get_barrier_semaphore()
    for a in range(n):
        for o in range(m):
            if a + o:
                pl.semaphore_signal(
                    barrier, inc=1, device_id=(lax.rem(me + a, n), lax.rem(slab + o, m)), device_id_type=MESH)

    shuf_a[...] = jnp.zeros_like(shuf_a)
    shuf_b[...] = jnp.zeros_like(shuf_b)
    des[...] = jnp.zeros_like(des)
    out_x[...] = jnp.zeros_like(out_x)
    for copy in small:
        copy.wait()

    row_high = lax.broadcasted_iota(jnp.int32, (16, BLOCK), 0) // 4
    left_half = lax.broadcasted_iota(jnp.int32, (4, HALF), 1) < QUARTER
    one = jnp.ones((), jnp.bfloat16)
    zero = jnp.zeros((), jnp.bfloat16)

    def shuffle(b, carry):
        at = pl.ds(pl.multiple_of(b * BLOCK, BLOCK), BLOCK)
        place = (
            lax.broadcasted_iota(jnp.int32, (QUARTER // 16, 16, BLOCK), 0) * 16
            + lax.broadcasted_iota(jnp.int32, (QUARTER // 16, 16, BLOCK), 1)
        ).astype(jnp.float32).astype(jnp.bfloat16)
        cov = cov_ref[:, at].astype(jnp.float32)
        for i in range(4):
            des[4 * i : 4 * i + 3, :] = cov
        des[16:17, :] = cov[0:1]
        des[17:18, :] = jnp.ones((1, BLOCK), jnp.float32)
        des[18:20, :] = cov[1:3]
        shuf_a[top : top + 4, :] = des[16:20, 0:HALF]
        shuf_b[top : top + 4, :] = des[16:20, HALF:BLOCK]
        des_all[:, at] = des[16:32, :].astype(jnp.bfloat16)

        local = perm_ref[:, at] & (BLOCK - 1)
        upper = local // QUARTER
        lower = (local & (QUARTER - 1)).astype(jnp.float32)
        base = des[0:16, :]
        for quad in range(copies // 4):
            lefts = []
            hots = []
            for p in range(4 * quad, 4 * quad + 4):
                lefts.append(jnp.where(upper[p : p + 1] == row_high, base, 0.0).astype(jnp.bfloat16))
                spread = jnp.broadcast_to(lower[p : p + 1], (16, BLOCK)).astype(jnp.bfloat16)
                hots.append(jnp.where(spread[None] == place, one, zero).reshape(QUARTER, BLOCK))
            left = jnp.concatenate(lefts, axis=0)
            hot = jnp.concatenate(hots, axis=0)
            moved = lax.dot_general(left, hot, NT, preferred_element_type=jnp.float32)
            for side in range(4):
                p = 4 * quad + side
                row = p // per * rows + p % per
                tile_lanes = slice(HALF * (side // 2), HALF * (side // 2) + HALF)
                for half, shuf in enumerate((shuf_a, shuf_b)):
                    first = 16 * side + 8 * half
                    part = moved[first : first + 8, tile_lanes]
                    turned = pltpu.roll(part, QUARTER, 1)
                    if side % 2 == 0:
                        joined = jnp.where(left_half, part[0:4], turned[4:8])
                    else:
                        joined = jnp.where(left_half, turned[0:4], part[4:8])
                    shuf[pl.ds(row, 3, stride=per), :] = joined[0:3]
        designs[:, at] = jnp.concatenate([shuf_a[...], shuf_b[...]], axis=1).astype(jnp.bfloat16)

        load(b).wait()
        cells = pl.ds(pl.multiple_of(b * span, span), span)
        flat[cells, :] = raw[cells, :].astype(jnp.float32)
        return carry

    lax.fori_loop(0, blocks, shuffle, 0)

    crossed = lax.dot_general(designs[...], des_all[...], NT, preferred_element_type=jnp.float32)
    for g in range(n):
        out_x[g, 0:rows, 0:16] = crossed[g * rows : (g + 1) * rows]
        out_x[g, rows:, 0:16] = crossed[top : top + 8]

    pl.semaphore_wait(barrier, n * m - 1)

    def exchange(src, dst, send_sem, recv_sem):
        made = []
        for o in range(1, n):
            to = lax.rem(me + o, n)
            made.append(pltpu.make_async_remote_copy(
                src_ref=src(to), dst_ref=dst(o), send_sem=send_sem(o), recv_sem=recv_sem(o),
                device_id=(to, slab), device_id_type=MESH))
            made[-1].start()
        return made

    copies_x = exchange(
        lambda g: out_x.at[g], lambda o: got_x.at[o], lambda o: xsend.at[o], lambda o: xrecv.at[o])
    got_x[0] = out_x[me]

    group = min(8, blocks)
    depth_k = group * BLOCK
    sub = lax.broadcasted_iota(jnp.int32, (8, wide), 0)
    per_slice = tiles // 2
    copies_t = []
    for tile in range(tiles):
        first_row = [2 * (2 * (tile % per_slice) + i) + tile // per_slice for i in range(2)]

        def multiply(k, carry):
            acc, sq = carry
            start = pl.multiple_of(k * depth_k * flat_rows, depth_k * flat_rows)
            part = jnp.concatenate(
                [flat[pl.ds(start + r, depth_k, stride=flat_rows), :] for r in first_row], axis=1)
            at = pl.ds(pl.multiple_of(k * depth_k, depth_k), depth_k)
            acc = acc + jnp.dot(
                designs[:, at], part.astype(jnp.bfloat16), preferred_element_type=jnp.float32)
            sq = sq + jnp.sum((part * part).reshape(depth_k // 8, 8, wide), axis=0)
            return acc, sq

        acc, sq = lax.fori_loop(
            0, blocks // group, multiply,
            (jnp.zeros((designs.shape[0], wide), jnp.float32), jnp.zeros((8, wide), jnp.float32)))
        squares = jnp.sum(sq, axis=0, keepdims=True)
        seen_rows = jnp.where(sub == 4, squares, acc[top : top + 8])
        for g in range(n):
            out[tile, g, 0:rows, :] = acc[g * rows : (g + 1) * rows]
            out[tile, g, rows:, :] = seen_rows
        copies_t.append(exchange(
            lambda g: out.at[tile, g], lambda o: got.at[tile, o],
            lambda o: send.at[tile, o], lambda o: recv.at[tile, o]))
        got[tile, 0] = out[tile, me]

    cells = mask_ref[...].astype(jnp.float32)
    mask_row = jnp.concatenate([cells[0:1], cells[1:2]], axis=1)

    def source(s):
        return lax.rem(me - s + n, n)

    for copy in copies_x:
        copy.wait()
    seen_x = got_x[source(0), rows:]
    for s in range(1, n):
        seen_x = seen_x + got_x[source(s), rows:]
    mine_x = got_x[0, 0:rows]
    for o in range(1, n):
        mine_x = mine_x + got_x[o, 0:rows]
    gram = [[seen_x[i : i + 1, j : j + 1] for j in range(4)] for i in range(4)]
    low_z = cholesky([row[1:4] for row in gram[1:4]])
    inv_z = [1.0 / low_z[i][i] for i in range(3)]
    low_f = cholesky(gram)
    inv_diag = [1.0 / low_f[i][i] for i in range(4)]
    unit = [jnp.zeros((1, 1), jnp.float32), jnp.ones((1, 1), jnp.float32)]
    columns = [cho_solve(low_f, inv_diag, [unit[int(i == j)] for i in range(4)]) for j in range(4)]
    inverse = [[columns[j][i] for j in range(4)] for i in range(4)]

    for tile in range(tiles):
        for copy in copies_t[tile]:
            copy.wait()
        cols = slice(tile * wide, (tile + 1) * wide)
        obs = got[tile, source(0), rows:]
        for s in range(1, n):
            obs = obs + got[tile, source(s), rows:]
        chunk = got[tile, 0, 0:rows]
        for o in range(1, n):
            chunk = chunk + got[tile, o, 0:rows]
        prod = [obs[k : k + 1] for k in range(4)]
        fit = cho_solve(low_z, inv_z, prod[1:4])
        resid = obs[4:5] - (prod[1] * fit[0] + prod[2] * fit[1] + prod[3] * fit[2])

        def statistic(proj):
            slope = sum(inverse[0][k] * proj[k] for k in range(4))
            quad = sum(proj[k] * sum(inverse[k][l] * proj[l] for l in range(4)) for k in range(4))
            return slope / jnp.sqrt((resid - quad) / freedom * inverse[0][0])

        seen = [prod[k] - sum(gram[k][1 + i] * fit[i] for i in range(3)) for k in range(4)]
        own_o[:, cols] = statistic(seen) * mask_row[:, cols]
        proj = []
        for c in range(3):
            at = slice(c * per, (c + 1) * per)
            proj.append(chunk[at] - sum(mine_x[at, 1 + i : 2 + i] * fit[i] for i in range(3)))
        own[:, cols] = statistic([proj[0], seen[1], proj[1], proj[2]]) * mask_row[:, cols]

    up = (me, lax.rem(slab + 1, m))
    down = (me, lax.rem(slab + m - 1, m))

    def halo(src, dst, k, to):
        return pltpu.make_async_remote_copy(
            src_ref=src, dst_ref=dst, send_sem=hsend.at[k], recv_sem=hrecv.at[k],
            device_id=to, device_id_type=MESH)

    rise = [halo(own, low, 0, up), halo(own_o, low_o, 1, up)]
    fall = [halo(own, high, 2, down), halo(own_o, high_o, 3, down)]

    @pl.when(slab < m - 1)
    def _():
        for copy in rise:
            copy.start()

    @pl.when(slab > 0)
    def _():
        for copy in fall:
            copy.start()

    @pl.when(slab == 0)
    def _():
        low[...] = jnp.zeros_like(low)
        low_o[...] = jnp.zeros_like(low_o)

    @pl.when(slab == m - 1)
    def _():
        high[...] = jnp.zeros_like(high)
        high_o[...] = jnp.zeros_like(high_o)

    field[...] = jnp.zeros_like(field)

    @pl.when(slab > 0)
    def _():
        for copy in rise:
            copy.wait_recv()

    @pl.when(slab < m - 1)
    def _():
        for copy in fall:
            copy.wait_recv()

    def deep(lower, mine, upper):
        slices = []
        for ref in (lower, mine, upper):
            value = ref[...]
            slices += [value[:, :plane], value[:, plane:]]
        return [
            sum(gauss_taps[position] * slices[position + z] for position in range(5))
            for z in range(2)
        ]

    first, second = deep(low, own, high)
    field[0:per, :] = first
    field[8 : 8 + per, :] = second
    first, second = deep(low_o, own_o, high_o)
    field[16:17, :] = first
    field[17:18, :] = second

    cell = lax.broadcasted_iota(jnp.int32, (24, plane), 1)
    smooth = blur(field[...], PY, cell // PY, PX)
    smooth = blur(smooth, 1, cell % PY, PY)

    peaks = jnp.maximum(
        jnp.max(jnp.where(cells[0:1] > 0, smooth[0:per] * cells[0:1], -1e30), axis=1, keepdims=True),
        jnp.max(jnp.where(cells[1:2] > 0, smooth[8 : 8 + per] * cells[1:2], -1e30), axis=1, keepdims=True),
    )
    pk1[0, 0] = jnp.broadcast_to(peaks, (per, LANES))
    copies_p = []
    for a in range(n):
        for o in range(m):
            if a + o:
                copies_p.append(pltpu.make_async_remote_copy(
                    src_ref=pk1.at[0, 0], dst_ref=pk1.at[a, o],
                    send_sem=psend.at[a, o], recv_sem=prec.at[a, o],
                    device_id=(lax.rem(me + a, n), lax.rem(slab + o, m)), device_id_type=MESH))
                copies_p[-1].start()
    seen_t = [smooth[16 + z : 17 + z] * cells[z : z + 1] for z in range(2)]
    smooth_ref[...] = jnp.concatenate(seen_t, axis=0)

    for copy in copies_p:
        copy.wait_recv()
    for a in range(n):
        best = pk1[a, 0]
        for o in range(1, m):
            best = jnp.maximum(best, pk1[a, o])
        peak_ref[lax.rem(me - a + n, n)] = best

    for copy in copies_p:
        copy.wait_send()

    @pl.when(slab < m - 1)
    def _():
        for copy in rise:
            copy.wait_send()

    @pl.when(slab > 0)
    def _():
        for copy in fall:
            copy.wait_send()


def p_kernel(smooth_ref, peaks_ref, mask_ref, t_ref, pval_ref, line_ref):
    n, per = peaks_ref.shape[:2]
    copies = n * per
    cells = mask_ref[...].astype(jnp.float32)
    values = smooth_ref[...]
    t_ref[...] = values
    line = jnp.zeros((1, LANES), jnp.float32)
    sub = lax.broadcasted_iota(jnp.int32, (per, LANES), 0)
    lane = lax.broadcasted_iota(jnp.int32, (per, LANES), 1)
    counts = [jnp.zeros((1, values.shape[1]), jnp.float32) for _ in range(2)]
    for d in range(n):
        value = peaks_ref[d]
        line = line + jnp.sum(jnp.where(lane == sub + d * per, value, 0.0), axis=0, keepdims=True)
        for z in range(2):
            level = jax.nn.sigmoid((value[:, 0:1] - values[z : z + 1]) / 0.2)
            counts[z] = counts[z] + jnp.sum(level, axis=0, keepdims=True)
    pval_ref[...] = cells * (1.0 + jnp.concatenate(counts, axis=0)) / (copies + 1)
    line_ref[...] = line[:, :copies]


def body(n, m, subjects_data, covariates, permutes, brain_mask):
    subj_rows, depth, plane = subjects_data.shape
    assert depth == 2 and plane == PX * PY
    copies = permutes.shape[0]
    per = copies // n
    rows = -(-3 * per // 8) * 8
    voxels = depth * plane
    wide = 2 * LANES
    tiles = voxels // wide
    lane_tiles = plane // LANES
    flat_rows = depth * lane_tiles
    data = (
        subjects_data.reshape(subj_rows, depth, lane_tiles, LANES)
        .transpose(0, 2, 1, 3)
        .reshape(subj_rows * flat_rows, LANES)
    )
    height = -(-(n * rows + 8) // 16) * 16
    f32 = jnp.float32
    bf16 = jnp.bfloat16
    vmem = pl.BlockSpec(memory_space=pltpu.VMEM)
    anywhere = pl.BlockSpec(memory_space=pl.ANY)
    dma = pltpu.SemaphoreType.DMA
    smooth, peaks = pl.pallas_call(
        functools.partial(maps_kernel, n, m, per, float(n * subj_rows - 4)),
        in_specs=[anywhere] * 4,
        out_specs=[vmem] * 2,
        out_shape=[
            jax.ShapeDtypeStruct((depth, plane), f32),
            jax.ShapeDtypeStruct((n, per, LANES), f32),
        ],
        scratch_shapes=[
            pltpu.VMEM((subj_rows * flat_rows, LANES), bf16),
            pltpu.VMEM((3, subj_rows), bf16),
            pltpu.VMEM((copies, subj_rows), jnp.int32),
            pltpu.VMEM((depth, plane), jnp.int32),
            pltpu.VMEM((subj_rows * flat_rows, LANES), f32),
            pltpu.VMEM((height, HALF), f32),
            pltpu.VMEM((height, HALF), f32),
            pltpu.VMEM((32, BLOCK), f32),
            pltpu.VMEM((16, subj_rows), bf16),
            pltpu.VMEM((height, subj_rows), bf16),
            pltpu.VMEM((n, rows + 8, LANES), f32),
            pltpu.VMEM((n, rows + 8, LANES), f32),
            pltpu.VMEM((tiles, n, rows + 8, wide), f32),
            pltpu.VMEM((tiles, n, rows + 8, wide), f32),
            pltpu.VMEM((per, voxels), f32),
            pltpu.VMEM((1, voxels), f32),
            pltpu.VMEM((per, voxels), f32),
            pltpu.VMEM((1, voxels), f32),
            pltpu.VMEM((per, voxels), f32),
            pltpu.VMEM((1, voxels), f32),
            pltpu.VMEM((24, plane), f32),
            pltpu.VMEM((n, m, per, LANES), f32),
            dma((subj_rows // BLOCK,)), dma((3,)), dma((n,)), dma((n,)),
            dma((tiles, n)), dma((tiles, n)),
            dma((4,)), dma((4,)), dma((n, m)), dma((n, m)),
        ],
        compiler_params=pltpu.CompilerParams(
            collective_id=0, has_side_effects=True, vmem_limit_bytes=60 * 2**20
        ),
        name="maps",
    )(data, covariates, permutes, brain_mask)
    smooth_t, p_values, line = pl.pallas_call(
        p_kernel,
        in_specs=[vmem] * 3,
        out_specs=[vmem] * 3,
        out_shape=[
            jax.ShapeDtypeStruct((depth, plane), f32),
            jax.ShapeDtypeStruct((depth, plane), f32),
            jax.ShapeDtypeStruct((1, copies), f32),
        ],
        name="p_values",
    )(smooth, peaks, brain_mask)
    return smooth_t, p_values, line.reshape(copies)


def solution(mesh):
    return jax.shard_map(
        functools.partial(body, mesh.shape["subj"], mesh.shape["slab"]),
        mesh=mesh,
        in_specs=(P("subj", "slab", None), P(None, "subj"), P(None, "subj"), P("slab", None)),
        out_specs=(P("slab", None), P("slab", None), P()),
        check_vma=False,
    )
```
